256 devices in a mesh: gz: 2 (over core), row: 4 (over x), col: 32 (over z, y).
Axes of the slice: x: 4, y: 4, z: 8, core: 2. Of those that a mesh axis runs over, the one named last changes fastest.
Arguments:
- ancestor: float32 [4096, 16384], P('row', 'col'), may hold values from -6 to 6
- lower_panel: bfloat16 [2, 64, 24, 128, 128], P('gz', 'col', 'row'), may hold values from -6 to 6
- row_ids: int32 [2, 64, 24], P('gz', 'col', 'row'), may hold values from 0 to 7, as said below
- row_counts: int32 [2, 64, 4], P('gz', 'col', 'row'), may hold values from 1 to 6
- diag_inverse: bfloat16 [2, 64, 128, 128], P('gz', 'col'), may hold values from -0.5 to 0.5
- upper_panel: bfloat16 [2, 64, 96, 128, 128], P('gz', 'row', 'col'), may hold values from -0.1875 to 0.1875
- col_ids: int32 [2, 64, 96], P('gz', 'row', 'col'), may hold values from 0 to 3, as said below
- col_counts: int32 [2, 64, 32], P('gz', 'row', 'col'), may hold values from 1 to 3
Outputs:
- updated: float32 [4096, 16384], P('row', 'col')
The draws below stay inside these ranges and needn't reach their ends.
Inputs may be any that keep to these rules, and one draw needn't show every extreme that they name: `row_ids`: within each layer, supernode and process row the 6 slots name distinct local block rows. `col_ids`: within each layer, supernode and process column the 3 slots name distinct local block columns.
All inputs are finite; a program needn't handle non-finite values.
Results may differ from the reference program's by a relative error of at most 0.0026.
Values may be sent and summed in bfloat16 or wider, within the bound.
A program may use at most 128 MiB of HBM per device.

```python
import jax
import jax.numpy as jnp
from jax import lax

B = 128
NAR_DEV = 8
NAC_DEV = 4
RL = 6
CL = 3
LAYERS = 2
KS = 64
RSLOTS = 24
CSLOTS = 96
NAR = 32
NAC = 128


def pick_subsets(key, leading, slots, pool):
    scores = jax.random.randint(key, leading + (pool,), 0, 1 << 20) * pool + jnp.arange(pool, dtype=jnp.int32)
    ranking = jnp.argsort(scores, axis=-1)
    return ranking[..., :slots].astype(jnp.int32)


def counts_reaching(key, shape, most):
    counts = jax.random.randint(jax.random.fold_in(key, 1), shape, 1, most + 1)
    flat = counts.reshape(-1)
    position = jax.random.randint(jax.random.fold_in(key, 2), (), 0, flat.shape[0])
    flat = flat.at[position].set(most)
    return flat.reshape(shape).astype(jnp.int32)


def draw_row_ids(key, part):
    groups = RSLOTS // RL
    chosen = pick_subsets(jax.random.fold_in(key, 11), (LAYERS, KS, groups), RL, NAR_DEV)
    return chosen.reshape(LAYERS, KS, RSLOTS)


def draw_row_counts(key, part):
    groups = RSLOTS // RL
    return counts_reaching(jax.random.fold_in(key, 12), (LAYERS, KS, groups), RL)


def draw_col_ids(key, part):
    groups = CSLOTS // CL
    chosen = pick_subsets(jax.random.fold_in(key, 21), (LAYERS, KS, groups), CL, NAC_DEV)
    return chosen.reshape(LAYERS, KS, CSLOTS)


def draw_col_counts(key, part):
    groups = CSLOTS // CL
    return counts_reaching(jax.random.fold_in(key, 22), (LAYERS, KS, groups), CL)


def levels(own_key, dims, cuts, least, top_value):
    factor_of = 1.0
    for axis_at, blocks in cuts:
        draws = jax.random.uniform(jax.random.fold_in(jax.random.fold_in(own_key, 6), axis_at), (blocks,), jnp.float32, least / len(cuts), top_value / len(cuts))
        factor_of = factor_of * jnp.repeat(jnp.exp(draws), dims[axis_at] // blocks).reshape((-1,) + (1,) * (len(dims) - 1 - axis_at))
    return factor_of


def normal_values(stream_key, dims, deviation, bound, pieces=(), held_as=jnp.bfloat16):
    array = deviation * jax.random.normal(stream_key, dims, jnp.float32)
    if pieces:
        array = array * levels(stream_key, dims, pieces, -0.22, 0.18)
    return jnp.clip(array, -bound, bound).astype(held_as)


def setup_inputs(seed: int = 0) -> dict:
    key_list = jax.random.split(jax.random.key(seed), 9)
    ancestor = normal_values(key_list[0], (NAR * B, NAC * B), 1.0, 6.0, ((0, 4), (1, 32)), jnp.float32)
    lower_panel = normal_values(key_list[1], (LAYERS, KS, RSLOTS, B, B), 1.0, 6.0, ((0, 2), (1, 32), (2, 4)))
    row_ids = draw_row_ids(jax.random.fold_in(key_list[8], 71), 0)
    row_counts = draw_row_counts(jax.random.fold_in(key_list[8], 71), 0)
    diag_inverse = normal_values(key_list[4], (LAYERS, KS, B, B), B ** -0.5, 0.5, ((0, 2), (1, 32)))
    upper_panel = normal_values(key_list[5], (LAYERS, KS, CSLOTS, B, B), (8 * B) ** -0.5, 0.1875, ((0, 2), (1, 4), (2, 32)))
    col_ids = draw_col_ids(jax.random.fold_in(key_list[8], 71), 0)
    col_counts = draw_col_counts(jax.random.fold_in(key_list[8], 71), 0)
    return dict(ancestor=ancestor, lower_panel=lower_panel, row_ids=row_ids, row_counts=row_counts, diag_inverse=diag_inverse, upper_panel=upper_panel, col_ids=col_ids, col_counts=col_counts)


def reference(ancestor, lower_panel, row_ids, row_counts, diag_inverse, upper_panel, col_ids, col_counts):
    highest = lax.Precision.HIGHEST
    slot_rows = jnp.arange(RSLOTS, dtype=jnp.int32)
    group_rows = slot_rows // RL
    slot_cols = jnp.arange(CSLOTS, dtype=jnp.int32)
    group_cols = slot_cols // CL
    updates = jnp.zeros((NAR, B, NAC, B), jnp.float32)
    for layer_index in range(LAYERS):
        def apply_one(accumulated, supernode_items):
            lower, rows, row_live, inverse, upper, cols, col_live = supernode_items
            solved = jnp.einsum('sab,bc->sac', lower.astype(jnp.float32), inverse.astype(jnp.float32), precision=highest)
            solved = lax.optimization_barrier(solved.astype(jnp.bfloat16)).astype(jnp.float32)
            alive_rows = (slot_rows % RL) < row_live[group_rows]
            solved = jnp.where(alive_rows[:, None, None], solved, jnp.float32(0.0))
            alive_cols = (slot_cols % CL) < col_live[group_cols]
            upper_live = jnp.where(alive_cols[:, None, None], upper.astype(jnp.float32), jnp.float32(0.0))
            tiles = jnp.einsum('sac,tcd->stad', solved, upper_live, precision=highest)
            global_rows = (group_rows * NAR_DEV + rows).astype(jnp.int32)
            global_cols = (group_cols * NAC_DEV + cols).astype(jnp.int32)
            accumulated = accumulated.at[global_rows[:, None], :, global_cols[None, :], :].add(tiles)
            return accumulated, None

        updates, _ = lax.scan(apply_one, updates, (lower_panel[layer_index], row_ids[layer_index], row_counts[layer_index], diag_inverse[layer_index], upper_panel[layer_index], col_ids[layer_index], col_counts[layer_index]))
    return ancestor - updates.reshape(NAR * B, NAC * B)
```

```python
import jax
import jax.numpy as jnp
from jax import lax
from jax.experimental import pallas as pl
from jax.experimental.pallas import tpu as pltpu
from jax.sharding import PartitionSpec as P

B = 128
RL = 6
CL = 3
RB = 8
CB = 4
NX, NY, NZ = 4, 4, 8
DEPTH = 16 * B
HALF = RB * B // 2
WIDE = CB * B
N_COPIES = 96
N_LOCAL = 16


def mod(value, size):
    return lax.rem(value + 2 * size, size)


def kernel(
    rid, rcnt, cid, ccnt, anc, low, dinv, up, out,
    lowv, dinvv, ancv, own_meta, relay_meta, meta_l, meta_u, ids_l, ids_u,
    lbuf, ubuf, relay_u, ld, ud, part_out, part_own, gz_in, c_out, c_in, c_relay, fin,
    send_sem, recv_sem, local_sem,
):
    g = lax.axis_index("gz")
    x = lax.axis_index("row")
    col = lax.axis_index("col")
    z = lax.div(col, NY)
    y = lax.rem(col, NY)
    f32, bf16 = jnp.float32, jnp.bfloat16

    xs = {d: mod(x + d, NX) for d in (-1, 1, 2)}
    ys = {d: mod(y + d, NY) for d in (-1, 1, 2)}
    zs = {d: mod(z + d, NZ) for d in (-3, -2, -1, 1, 2, 3, 4)}
    xs[0], ys[0], zs[0] = x, y, z

    def place(axis, d):
        if axis == "x":
            return {"gz": g, "row": xs[d], "col": col}
        if axis == "y":
            return {"gz": g, "row": x, "col": z * NY + ys[d]}
        if axis == "z":
            return {"gz": g, "row": x, "col": zs[d] * NY + y}
        return {"gz": 1 - g, "row": x, "col": col}

    started = []
    count = [0]
    locals_started = [0]

    class Copy:
        def __init__(self, src, dst, axis, d):
            at = count[0]
            count[0] += 1
            self.copy = pltpu.make_async_remote_copy(
                src_ref=src, dst_ref=dst, send_sem=send_sem.at[at], recv_sem=recv_sem.at[at],
                device_id=place(axis, d), device_id_type=pl.DeviceIdType.MESH,
            )
            self.copy.start()
            started.append(self.copy)

        def arrived(self):
            self.copy.wait_recv()

    def local(src, dst):
        copy = pltpu.make_async_copy(src, dst, local_sem.at[locals_started[0]])
        locals_started[0] += 1
        copy.start()
        return copy

    mine = pl.ds(pl.multiple_of(g * HALF, HALF), HALF)
    theirs = pl.ds(pl.multiple_of((1 - g) * HALF, HALF), HALF)

    get_low = local(low, lowv)
    get_dinv = local(dinv, dinvv)
    get_up = local(up.at[:, y], ubuf.at[y, x])
    get_anc = local(anc.at[mine], ancv)

    barrier = pltpu.get_barrier_semaphore()
    for axis, d in (("x", 1), ("x", -1), ("y", 1), ("y", -1), ("z", 1), ("z", -1), ("g", 1)):
        pl.semaphore_signal(barrier, 1, device_id=place(axis, d), device_id_type=pl.DeviceIdType.MESH)

    lane = lax.broadcasted_iota(jnp.int32, (1, B), 1)
    row_list = jnp.full((1, B), RB, jnp.int32)
    for b in range(2):
        for s in range(RL):
            value = jnp.where(s < rcnt[b, 0], rid[b, s], RB)
            row_list = jnp.where(lane == b * RL + s, value, row_list)
    meta_l[z] = row_list
    for q in range(NY):
        col_list = jnp.full((1, B), CB, jnp.int32)
        for zz in range(2):
            for b in range(2):
                k = zz * 8 + q * 2 + b
                for s in range(CL):
                    value = jnp.where(s < ccnt[k, 0], cid[k, s], CB)
                    col_list = jnp.where(lane == (zz * 2 + b) * CL + s, value, col_list)
        own_meta[q] = col_list
    meta_u[x, y] = own_meta[y]

    get_low.wait()
    get_dinv.wait()
    for b in range(2):
        solved = jnp.dot(
            lowv[b].reshape(RL * B, B), dinvv[b], preferred_element_type=f32
        ).astype(bf16)
        lbuf[z, b] = solved.reshape(RL, B, B)

    pl.semaphore_wait(barrier, 7)

    both = (1, -1)
    half_of = {1: 0, -1: 1}
    my = {d: Copy(own_meta.at[ys[d]], meta_u.at[x, y], "y", d) for d in both}
    my_far = Copy(own_meta.at[ys[2]], relay_meta, "y", 1)
    ml = {(d, 0): Copy(meta_l.at[z], meta_l.at[z], "z", d) for d in both}
    yr = {d: Copy(up.at[half_of[d], ys[2]], relay_u.at[half_of[d]], "y", d) for d in both}
    lz = {(d, 0, b): Copy(lbuf.at[z, b], lbuf.at[z, b], "z", d) for b in range(2) for d in both}
    xo = {}
    for h in range(2):
        for d in both:
            xo[d, 0, h] = Copy(up.at[h, y], ubuf.at[y, x, h], "x", d)
    yd = {
        (d, h): Copy(up.at[h, ys[d]], ubuf.at[y, x, h], "y", d) for h in range(2) for d in both
    }
    get_up.wait()

    def forward_list(d, hop):
        ml[d, hop] = Copy(meta_l.at[zs[-d * hop]], meta_l.at[zs[-d * hop]], "z", d)

    def forward_lower(d, hop, b):
        lz[d, hop, b] = Copy(lbuf.at[zs[-d * hop], b], lbuf.at[zs[-d * hop], b], "z", d)

    def along_x(block, h):
        for d in both:
            xo[d, block, h] = Copy(ubuf.at[ys[block], x, h], ubuf.at[ys[block], x, h], "x", d)

    xf = {}

    def onward_x(block):
        for d in both:
            h = half_of[d]
            xf[d, block] = Copy(
                ubuf.at[ys[block], xs[-d], h], ubuf.at[ys[block], xs[-d], h], "x", d
            )

    for d in both:
        my[d].arrived()
        ml[d, 0].arrived()
        forward_list(d, 1)
    my_far.arrived()
    far_list = Copy(relay_meta, meta_u.at[x, ys[-1]], "y", 1)
    for d in both:
        lz[d, 0, 0].arrived()
        forward_lower(d, 1, 0)
    yrf = {}
    for d in both:
        yr[d].arrived()
        yrf[d] = Copy(relay_u.at[half_of[d]], ubuf.at[ys[-d], x, half_of[d]], "y", d)
    for d in both:
        ml[d, 1].arrived()
        forward_list(d, 2)
        lz[d, 0, 1].arrived()
        forward_lower(d, 1, 1)
    far_list.arrived()
    mx = {d: Copy(meta_u.at[x], meta_u.at[x], "x", d) for d in both}
    yd[1, 0].arrived()
    yd[-1, 0].arrived()
    along_x(-1, 0)
    along_x(1, 0)
    for d in both:
        lz[d, 1, 0].arrived()
        forward_lower(d, 2, 0)
        ml[d, 2].arrived()
    forward_list(1, 3)
    yd[1, 1].arrived()
    yd[-1, 1].arrived()
    along_x(-1, 1)
    along_x(1, 1)
    for d in both:
        mx[d].arrived()
    mx_far = Copy(meta_u.at[xs[-1]], meta_u.at[xs[-1]], "x", 1)
    for d in both:
        lz[d, 1, 1].arrived()
        forward_lower(d, 2, 1)
    for d in both:
        yrf[d].arrived()
    for d in both:
        lz[d, 2, 0].arrived()
    forward_lower(1, 3, 0)
    ml[1, 3].arrived()
    get_ids_l = local(meta_l, ids_l)
    for h in range(2):
        for d in both:
            xo[d, -1, h].arrived() if h == 0 else None
    for d in both:
        xo[d, 1, 0].arrived()
    for d in both:
        xo[d, -1, 1].arrived()
    onward_x(-1)
    for d in both:
        lz[d, 2, 1].arrived()
    forward_lower(-1, 3, 1)
    mx_far.arrived()
    get_ids_u = local(meta_u, ids_u)
    for d in both:
        xo[d, 1, 1].arrived()
    onward_x(1)
    along_x(2, 0)
    along_x(2, 1)
    for d in both:
        for h in range(2):
            xo[d, 0, h].arrived()
    get_ids_l.wait()
    lz[1, 3, 0].arrived()
    lz[-1, 3, 1].arrived()

    @pl.loop(0, NZ)
    def _(zi):
        for b in range(2):
            ids = [ids_l[zi, 0, b * RL + s] for s in range(RL)]
            at = pl.ds(pl.multiple_of(zi * 2 * B + b * B, B), B)
            for i in range(RB):
                tile = jnp.zeros((B, B), bf16)
                for s in range(RL):
                    tile = lax.select(ids[s] == i, lbuf[zi, b, s], tile)
                ld[i * B : (i + 1) * B, at] = tile

    get_ids_u.wait()

    def spread_upper(block, xi):
        for h in range(2):
            for b in range(2):
                k = h * 2 + b
                ids = [ids_u[xi, block, 0, k * CL + s] for s in range(CL)]
                at = pl.ds(pl.multiple_of(xi * 4 * B + k * B, B), B)
                for j in range(CB):
                    tile = jnp.zeros((B, B), bf16)
                    for s in range(CL):
                        tile = lax.select(ids[s] == j, ubuf[block, xi, h, b * CL + s], tile)
                    ud[at, j * B : (j + 1) * B] = tile

    def multiply(rows):
        return jnp.dot(ld[rows, :], ud[...], preferred_element_type=f32)

    gz = {}

    def contribute(block, at):
        @pl.loop(0, NX)
        def _(xi):
            spread_upper(ys[block], xi)

        part_out[at] = multiply(theirs)
        part_own[at] = multiply(mine)
        gz[at] = Copy(part_out.at[at], gz_in.at[at], "g", 1)

    cs = {}

    def settle(block, at):
        gz[at].arrived()
        c_out[at] = (part_own[at] + gz_in[at]).astype(bf16)
        if block == 2:
            for d in both:
                for n in range(2):
                    rows = pl.ds((2 * half_of[d] + n) * B, B)
                    cs[d, n] = Copy(c_out.at[at, rows], c_relay.at[rows], "y", d)
        else:
            cs[block] = Copy(c_out.at[at], c_in.at[at], "y", block)

    for d in both:
        xf[d, -1].arrived()
    contribute(-1, 0)
    for d in both:
        for h in range(2):
            xo[d, 2, h].arrived()
    onward_x(2)
    onward_x(0)
    for d in both:
        xf[d, 1].arrived()
    settle(-1, 0)
    contribute(1, 1)
    settle(1, 1)

    for d in both:
        xf[d, 2].arrived()
    contribute(2, 2)
    settle(2, 2)
    for d in both:
        xf[d, 0].arrived()
    contribute(0, 3)

    cf = {}
    for n in range(2):
        for d in both:
            rows = pl.ds((2 * half_of[d] + n) * B, B)
            cs[d, n].arrived()
            cf[d, n] = Copy(c_relay.at[rows], c_in.at[2, rows], "y", d)
    gz[3].arrived()
    cs[-1].arrived()
    cs[1].arrived()
    get_anc.wait()
    fin[...] = ancv[...] - (part_own[3] + gz_in[3] + c_in[0].astype(f32) + c_in[1].astype(f32))
    last = []
    stores = []
    for n in range(2):
        for d in both:
            begin = (2 * half_of[d] + n) * B
            rows = pl.ds(begin, B)
            there = pl.ds(pl.multiple_of(g * HALF + begin, B), B)
            cf[d, n].arrived()
            fin[rows] = fin[rows] - c_in[2, rows].astype(f32)
            stores.append(local(fin.at[rows], out.at[there]))
            last.append(Copy(fin.at[rows], out.at[there], "g", 1))
    for copy in last:
        copy.arrived()
    for store in stores:
        store.wait()
    for copy in started:
        copy.wait_send()


def on_device(
    ancestor, lower_panel, row_ids, row_counts, diag_inverse, upper_panel, col_ids, col_counts
):
    bf16, f32, i32 = jnp.bfloat16, jnp.float32, jnp.int32
    anywhere = pl.BlockSpec(memory_space=pl.ANY)
    scalars = pl.BlockSpec(memory_space=pltpu.SMEM)
    vmem = pltpu.VMEM
    return pl.pallas_call(
        kernel,
        out_shape=jax.ShapeDtypeStruct(ancestor.shape, f32),
        in_specs=[scalars] * 4 + [anywhere] * 4,
        out_specs=anywhere,
        scratch_shapes=[
            vmem((2, RL, B, B), bf16),
            vmem((2, B, B), bf16),
            vmem((HALF, WIDE), f32),
            vmem((NY, 1, B), i32),
            vmem((1, B), i32),
            vmem((NZ, 1, B), i32),
            vmem((NX, NY, 1, B), i32),
            pltpu.SMEM((NZ, 1, B), i32),
            pltpu.SMEM((NX, NY, 1, B), i32),
            vmem((NZ, 2, RL, B, B), bf16),
            vmem((NY, NX, 2, 2 * CL, B, B), bf16),
            vmem((2, 2 * CL, B, B), bf16),
            vmem((RB * B, DEPTH), bf16),
            vmem((DEPTH, WIDE), bf16),
            vmem((4, HALF, WIDE), f32),
            vmem((4, HALF, WIDE), f32),
            vmem((4, HALF, WIDE), f32),
            vmem((3, HALF, WIDE), bf16),
            vmem((3, HALF, WIDE), bf16),
            vmem((HALF, WIDE), bf16),
            vmem((HALF, WIDE), f32),
            pltpu.SemaphoreType.DMA((N_COPIES,)),
            pltpu.SemaphoreType.DMA((N_COPIES,)),
            pltpu.SemaphoreType.DMA((N_LOCAL,)),
        ],
        compiler_params=pltpu.CompilerParams(
            collective_id=0, has_side_effects=True, vmem_limit_bytes=60 * 1024 * 1024
        ),
        name="schur_update",
    )(
        row_ids[0], row_counts[0], col_ids[0], col_counts[0],
        ancestor, lower_panel[0], diag_inverse[0],
        upper_panel[0].reshape(2, NY, 2 * CL, B, B),
    )


def solution(mesh):
    placed = (
        P("row", "col"),
        P("gz", "col", "row", None, None),
        P("gz", "col", "row"),
        P("gz", "col", "row"),
        P("gz", "col", None, None),
        P("gz", "row", "col", None, None),
        P("gz", "row", "col"),
        P("gz", "row", "col"),
    )
    return jax.shard_map(
        on_device, mesh=mesh, in_specs=placed, out_specs=P("row", "col"), check_vma=False
    )
```

```python
import jax
import jax.numpy as jnp
from jax import lax
from jax.experimental import pallas as pl
from jax.experimental.pallas import tpu as pltpu
from jax.sharding import PartitionSpec as P

B = 128
RL = 6
CL = 3
RB = 8
CB = 4
NX, NY, NZ = 4, 4, 8
DEPTH = 16 * B
HALF = RB * B // 2
WIDE = CB * B
N_COPIES = 112
N_LOCAL = 16


def mod(value, size):
    return lax.rem(value + 2 * size, size)


def kernel(
    rid, rcnt, cid, ccnt, anc, low, dinv, up, out,
    lowv, dinvv, ancv, own_meta, relay_meta, meta_l, meta_u, ids_l, ids_u,
    lbuf, ubuf, relay_u, ld, ud, part_out, part_own, gz_in, c_out, c_in, c_relay, fin,
    send_sem, recv_sem, local_sem,
):
    g = lax.axis_index("gz")
    x = lax.axis_index("row")
    col = lax.axis_index("col")
    z = lax.div(col, NY)
    y = lax.rem(col, NY)
    f32, bf16 = jnp.float32, jnp.bfloat16

    xs = {d: mod(x + d, NX) for d in (-1, 1, 2)}
    ys = {d: mod(y + d, NY) for d in (-1, 1, 2)}
    zs = {d: mod(z + d, NZ) for d in (-3, -2, -1, 1, 2, 3, 4)}
    xs[0], ys[0], zs[0] = x, y, z

    def place(axis, d):
        if axis == "x":
            return {"gz": g, "row": xs[d], "col": col}
        if axis == "y":
            return {"gz": g, "row": x, "col": z * NY + ys[d]}
        if axis == "z":
            return {"gz": g, "row": x, "col": zs[d] * NY + y}
        return {"gz": 1 - g, "row": x, "col": col}

    started = []
    count = [0]
    locals_started = [0]

    class Copy:
        def __init__(self, src, dst, axis, d):
            at = count[0]
            count[0] += 1
            self.copy = pltpu.make_async_remote_copy(
                src_ref=src, dst_ref=dst, send_sem=send_sem.at[at], recv_sem=recv_sem.at[at],
                device_id=place(axis, d), device_id_type=pl.DeviceIdType.MESH,
            )
            self.copy.start()
            started.append(self.copy)

        def arrived(self):
            self.copy.wait_recv()

    def local(src, dst):
        copy = pltpu.make_async_copy(src, dst, local_sem.at[locals_started[0]])
        locals_started[0] += 1
        copy.start()
        return copy

    mine = pl.ds(pl.multiple_of(g * HALF, HALF), HALF)
    theirs = pl.ds(pl.multiple_of((1 - g) * HALF, HALF), HALF)

    get_low = local(low, lowv)
    get_dinv = local(dinv, dinvv)
    get_up = local(up.at[:, y], ubuf.at[y, x])
    get_anc = local(anc.at[mine], ancv)

    barrier = pltpu.get_barrier_semaphore()
    for axis, d in (("x", 1), ("x", -1), ("y", 1), ("y", -1), ("z", 1), ("z", -1), ("g", 1)):
        pl.semaphore_signal(barrier, 1, device_id=place(axis, d), device_id_type=pl.DeviceIdType.MESH)

    lane = lax.broadcasted_iota(jnp.int32, (1, B), 1)
    row_list = jnp.full((1, B), RB, jnp.int32)
    for b in range(2):
        for s in range(RL):
            value = jnp.where(s < rcnt[0, b], rid[b, s], RB)
            row_list = jnp.where(lane == b * RL + s, value, row_list)
    meta_l[z] = row_list
    for q in range(NY):
        col_list = jnp.full((1, B), CB, jnp.int32)
        for zz in range(2):
            for b in range(2):
                k = zz * 8 + q * 2 + b
                for s in range(CL):
                    value = jnp.where(s < ccnt[0, k], cid[s, 0, k], CB)
                    col_list = jnp.where(lane == (zz * 2 + b) * CL + s, value, col_list)
        own_meta[q] = col_list
    meta_u[x, y] = own_meta[y]


    pl.semaphore_wait(barrier, 7)

    both = (1, -1)
    half_of = {1: 0, -1: 1}
    my = {d: Copy(own_meta.at[ys[d]], meta_u.at[x, y], "y", d) for d in both}
    my_far = Copy(own_meta.at[ys[2]], relay_meta, "y", 1)
    ml = {(d, 0): Copy(meta_l.at[z], meta_l.at[z], "z", d) for d in both}
    xo, xf, yd = {}, {}, {}
    for d in both:
        h = half_of[d]
        xo[d, 0, h] = Copy(up.at[h, y], ubuf.at[y, x, h], "x", d)
        yd[d, 0] = Copy(up.at[1 - h, ys[d]], ubuf.at[y, x, 1 - h], "y", d)
    own_late = {}
    for d in both:
        h = 1 - half_of[d]
        xo[d, 0, h] = Copy(up.at[h, y, 0:CL], ubuf.at[y, x, h, 0:CL], "x", d)

    get_low.wait()
    get_dinv.wait()
    for b in range(2):
        solved = jnp.dot(
            lowv[b].reshape(RL * B, B), dinvv[b], preferred_element_type=f32
        ).astype(bf16)
        lbuf[z, b] = solved.reshape(RL, B, B)
    lz = {(d, 0, b): Copy(lbuf.at[z, b], lbuf.at[z, b], "z", d) for b in range(2) for d in both}
    my_far.arrived()
    far_list = Copy(relay_meta, meta_u.at[x, ys[-1]], "y", 1)
    for d in both:
        h = half_of[d]
        yd[d, 1] = Copy(up.at[h, ys[d]], ubuf.at[y, x, h], "y", d)
    yr = {d: Copy(up.at[half_of[d], ys[2]], relay_u.at[half_of[d]], "y", d) for d in both}
    get_up.wait()

    def forward_list(d, hop):
        ml[d, hop] = Copy(meta_l.at[zs[-d * hop]], meta_l.at[zs[-d * hop]], "z", d)

    def forward_lower(d, hop, b):
        lz[d, hop, b] = Copy(lbuf.at[zs[-d * hop], b], lbuf.at[zs[-d * hop], b], "z", d)

    def along_x(d, block, h):
        xo[d, block, h] = Copy(ubuf.at[ys[block], x, h], ubuf.at[ys[block], x, h], "x", d)

    def onward_x(d, block):
        h = half_of[d]
        xo[d, block, h].arrived()
        xf[d, block] = Copy(ubuf.at[ys[block], xs[-d], h], ubuf.at[ys[block], xs[-d], h], "x", d)

    for d in both:
        my[d].arrived()
        ml[d, 0].arrived()
        forward_list(d, 1)
    for d in both:
        lz[d, 0, 0].arrived()
        forward_lower(d, 1, 0)
    for d in both:
        yd[d, 0].arrived()
        along_x(-d, -d, 1 - half_of[d])
    far_list.arrived()
    mx = {d: Copy(meta_u.at[x], meta_u.at[x], "x", d) for d in both}
    for d in both:
        ml[d, 1].arrived()
        forward_list(d, 2)
        lz[d, 0, 1].arrived()
        forward_lower(d, 1, 1)
    for d in both:
        yd[d, 1].arrived()
    for d in both:
        along_x(d, -d, half_of[d])
    for d in both:
        along_x(d, d, 1 - half_of[d])
    for d in both:
        mx[d].arrived()
    mx_far = Copy(meta_u.at[xs[-1]], meta_u.at[xs[-1]], "x", 1)
    for d in both:
        along_x(d, -d, 1 - half_of[d])
    for d in both:
        lz[d, 1, 0].arrived()
        forward_lower(d, 2, 0)
        ml[d, 2].arrived()
    forward_list(1, 3)
    yrf = {}
    for d in both:
        yr[d].arrived()
        yrf[d] = Copy(relay_u.at[half_of[d]], ubuf.at[ys[-d], x, half_of[d]], "y", d)
    for d in both:
        onward_x(d, d)
    for d in both:
        lz[d, 1, 1].arrived()
        forward_lower(d, 2, 1)
    for d in both:
        onward_x(d, -d)
    for d in both:
        yrf[d].arrived()
    for d in both:
        along_x(d, 2, half_of[d])
    for d in both:
        along_x(d, 2, 1 - half_of[d])
    for d in both:
        lz[d, 2, 0].arrived()
    forward_lower(1, 3, 0)
    ml[1, 3].arrived()
    get_ids_l = local(meta_l, ids_l)
    for d in both:
        lz[d, 2, 1].arrived()
    forward_lower(-1, 3, 1)
    mx_far.arrived()
    get_ids_u = local(meta_u, ids_u)
    get_ids_l.wait()

    def spread_lower(zi):
        for b in range(2):
            ids = [ids_l[zi, 0, b * RL + s] for s in range(RL)]
            at = pl.ds(pl.multiple_of(zi * 2 * B + b * B, B), B)
            for i in range(RB):
                tile = jnp.zeros((B, B), bf16)
                for s in range(RL):
                    tile = lax.select(ids[s] == i, lbuf[zi, b, s], tile)
                ld[i * B : (i + 1) * B, at] = tile

    @pl.loop(1, NZ)
    def _(hop):
        spread_lower(mod(z + hop - 4 - NZ, NZ))

    get_ids_u.wait()

    def spread_upper(block, xi):
        for h in range(2):
            for b in range(2):
                k = h * 2 + b
                ids = [ids_u[xi, block, 0, k * CL + s] for s in range(CL)]
                at = pl.ds(pl.multiple_of(xi * 4 * B + k * B, B), B)
                for j in range(CB):
                    tile = jnp.zeros((B, B), bf16)
                    for s in range(CL):
                        tile = lax.select(ids[s] == j, ubuf[block, xi, h, b * CL + s], tile)
                    ud[at, j * B : (j + 1) * B] = tile

    def multiply(rows):
        return jnp.dot(ld[rows, :], ud[...], preferred_element_type=f32)

    def multiply_part(rows, xi):
        depth = pl.ds(pl.multiple_of(xi * 4 * B, 4 * B), 4 * B)
        return jnp.dot(ld[rows, depth], ud[depth, :], preferred_element_type=f32)

    gz = {}
    cs = {}

    def contribute(block, at):
        @pl.loop(0, NX)
        def _(xi):
            spread_upper(ys[block], xi)

        part_out[at] = multiply(theirs)
        part_own[at] = multiply(mine)
        gz[at] = Copy(part_out.at[at], gz_in.at[at], "g", 1)

    def begin(block, at):
        @pl.loop(0, NX - 1)
        def _(n):
            spread_upper(ys[block], mod(x + n - 1, NX))

        for rows, part in ((theirs, part_out), (mine, part_own)):
            part[at] = (
                multiply_part(rows, xs[-1]) + multiply_part(rows, x) + multiply_part(rows, xs[1])
            )

    def settle(block, at):
        gz[at].arrived()
        c_out[at] = (part_own[at] + gz_in[at]).astype(bf16)
        cs[block] = Copy(c_out.at[at], c_in.at[at], "y", block)

    lz[1, 3, 0].arrived()
    lz[-1, 3, 1].arrived()
    spread_lower(zs[4])
    for d in both:
        xo[d, d, 1 - half_of[d]].arrived()
        xo[d, -d, 1 - half_of[d]].arrived()
    for d in both:
        xf[d, 1].arrived()
    contribute(1, 1)
    for d in both:
        xf[d, -1].arrived()
    contribute(-1, 0)
    for d in both:
        onward_x(d, 2)
    for d in both:
        h = 1 - half_of[d]
        own_late[d] = Copy(up.at[h, y, CL:], ubuf.at[y, x, h, CL:], "x", d)
    for d in both:
        onward_x(d, 0)
    settle(1, 1)
    settle(-1, 0)
    for d in both:
        xo[d, 2, 1 - half_of[d]].arrived()
    begin(2, 2)

    def chunk(d, p, m):
        return p * 2 * B + half_of[d] * B + m * (B // 2)

    for d in both:
        xf[d, 2].arrived()
    spread_upper(ys[2], xs[2])
    pieces = [pl.ds(p * 2 * B, 2 * B) for p in range(2)]

    def piece_of(side, p):
        return pl.ds(pl.multiple_of(side * HALF + p * 2 * B, 2 * B), 2 * B)

    for p in range(2):
        part_out[2, pieces[p]] += multiply_part(piece_of(1 - g, p), xs[2])
    for p in range(2):
        gz[2, p] = Copy(part_out.at[2, pieces[p]], gz_in.at[2, pieces[p]], "g", 1)
    for p in range(2):
        part_own[2, pieces[p]] += multiply_part(piece_of(g, p), xs[2])
    for p in range(2):
        gz[2, p].arrived()
        c_out[2, pieces[p]] = (part_own[2, pieces[p]] + gz_in[2, pieces[p]]).astype(bf16)
        for m in range(2):
            for d in both:
                rows = pl.ds(chunk(d, p, m), B // 2)
                cs[d, p, m] = Copy(c_out.at[2, rows], c_relay.at[rows], "y", d)
    for d in both:
        xo[d, 0, 1 - half_of[d]].arrived()
        own_late[d].arrived()
    begin(0, 3)
    for d in both:
        xf[d, 0].arrived()
    spread_upper(y, xs[2])
    part_out[3] += multiply_part(theirs, xs[2])
    part_own[3] += multiply_part(mine, xs[2])
    gz[3] = Copy(part_out.at[3], gz_in.at[3], "g", 1)

    cf = {}
    for p in range(2):
        for m in range(2):
            for d in both:
                rows = pl.ds(chunk(d, p, m), B // 2)
                cs[d, p, m].arrived()
                cf[d, p, m] = Copy(c_relay.at[rows], c_in.at[2, rows], "y", d)
    cs[-1].arrived()
    cs[1].arrived()
    gz[3].arrived()
    get_anc.wait()
    fin[...] = ancv[...] - (part_own[3] + gz_in[3] + c_in[0].astype(f32) + c_in[1].astype(f32))
    last = []
    for p in range(2):
        for m in range(2):
            for d in both:
                begins = chunk(d, p, m)
                rows = pl.ds(begins, B // 2)
                there = pl.ds(pl.multiple_of(g * HALF + begins, B // 2), B // 2)
                cf[d, p, m].arrived()
                out[there] = fin[rows] - c_in[2, rows].astype(f32)
                last.append(Copy(out.at[there], out.at[there], "g", 1))
    for copy in last:
        copy.arrived()
    for copy in started:
        copy.wait_send()


def on_device(
    ancestor, lower_panel, row_ids, row_counts, diag_inverse, upper_panel, col_ids, col_counts
):
    bf16, f32, i32 = jnp.bfloat16, jnp.float32, jnp.int32
    anywhere = pl.BlockSpec(memory_space=pltpu.HBM)
    scalars = pl.BlockSpec(memory_space=pltpu.SMEM)
    vmem = pltpu.VMEM
    return pl.pallas_call(
        kernel,
        out_shape=pltpu.VMEM(ancestor.shape, f32),
        in_specs=[scalars] * 4 + [anywhere] * 4,
        out_specs=pl.BlockSpec(memory_space=pltpu.VMEM),
        scratch_shapes=[
            vmem((2, RL, B, B), bf16),
            vmem((2, B, B), bf16),
            vmem((HALF, WIDE), f32),
            vmem((NY, 1, B), i32),
            vmem((1, B), i32),
            vmem((NZ, 1, B), i32),
            vmem((NX, NY, 1, B), i32),
            pltpu.SMEM((NZ, 1, B), i32),
            pltpu.SMEM((NX, NY, 1, B), i32),
            vmem((NZ, 2, RL, B, B), bf16),
            vmem((NY, NX, 2, 2 * CL, B, B), bf16),
            vmem((2, 2 * CL, B, B), bf16),
            vmem((RB * B, DEPTH), bf16),
            vmem((DEPTH, WIDE), bf16),
            vmem((4, HALF, WIDE), f32),
            vmem((4, HALF, WIDE), f32),
            vmem((4, HALF, WIDE), f32),
            vmem((3, HALF, WIDE), bf16),
            vmem((3, HALF, WIDE), bf16),
            vmem((HALF, WIDE), bf16),
            vmem((HALF, WIDE), f32),
            pltpu.SemaphoreType.DMA((N_COPIES,)),
            pltpu.SemaphoreType.DMA((N_COPIES,)),
            pltpu.SemaphoreType.DMA((N_LOCAL,)),
        ],
        compiler_params=pltpu.CompilerParams(
            collective_id=0, has_side_effects=True, vmem_limit_bytes=64_800_000
        ),
        name="schur_update",
    )(
        row_ids[0], row_counts.reshape(1, -1), col_ids.transpose(2, 0, 1), col_counts.reshape(1, -1),
        ancestor, lower_panel[0], diag_inverse[0],
        upper_panel[0].reshape(2, NY, 2 * CL, B, B),
    )


def solution(mesh):
    placed = (
        P("row", "col"),
        P("gz", "col", "row", None, None),
        P("gz", "col", "row"),
        P("gz", "col", "row"),
        P("gz", "col", None, None),
        P("gz", "row", "col", None, None),
        P("gz", "row", "col"),
        P("gz", "row", "col"),
    )
    return jax.shard_map(
        on_device, mesh=mesh, in_specs=placed, out_specs=P("row", "col"), check_vma=False
    )
```
